32 devices in a mesh: groups: 2 (over y), hx: 16 (over z, x, core).
Axes of the slice: x: 2, y: 2, z: 4, core: 2. Of those that a mesh axis runs over, the one named last changes fastest.
Arguments:
- tokens: bfloat16 [32, 8192], P(('groups', 'hx')), parts along dimension 0, may hold values from -6 to 6
- gate_codes: bfloat16 [8192, 26624], P(None, 'hx'), may hold values from -8 to 7, as said below
- gate_scales: float32 [64, 26624], P(None, 'hx'), may hold values from 0.00077339803 to 0.00773398
- up_codes: bfloat16 [8192, 26624], P(None, 'hx'), may hold values from -8 to 7, as said below
- up_scales: float32 [64, 26624], P(None, 'hx'), may hold values from 0.00077339803 to 0.00773398
- down_codes: bfloat16 [26624, 8192], P('hx'), may hold values from -8 to 7, as said below
- down_scales: float32 [8192], replicated, may hold values from 0.00061286293 to 0.006128629
- hadamard: int32 [52, 52], replicated, may hold values from -1 to 1, as said below
Outputs:
- mixed: bfloat16 [32, 8192], P(('groups', 'hx')), parts along dimension 0
The draws below stay inside these ranges and needn't reach their ends.
There are 2 independent parts, one for each index of `groups`. The reference program is written for one: setup_inputs(seed, part) draws one part's arguments, and reference() takes and returns one part's arrays. A program takes and returns all parts, laid end to end along the dimension named above; an argument that names none is the same for every part. Nothing has to cross between parts.
Inputs may be any that keep to these rules, and one draw needn't show every extreme that they name: `gate_codes`: whole numbers. `up_codes`: whole numbers. `down_codes`: whole numbers. `hadamard`: a Hadamard matrix: every entry is -1 or 1 and any two rows are orthogonal.
All inputs are finite; a program needn't handle non-finite values.
Results may differ from the reference program's by a relative error of at most 0.015.
Values may be sent and summed in bfloat16 or wider, within the bound.
A program may use at most 192 MiB of HBM per device.

```python
import math
import jax
import jax.numpy as jnp
import numpy as np
from jax import lax

D = 8192
HA = 512
HB = 52
GROUP = 128
FF = 26624
TOKENS = 16


def field_product(left, right):
    return ((left[0] * right[0] + 2 * left[1] * right[1]) % 5, (left[0] * right[1] + left[1] * right[0]) % 5)


def paley_table():
    members = [(first, second) for first in range(5) for second in range(5)]
    squares = set()
    for member in members:
        if member != (0, 0):
            squares.add(field_product(member, member))
    count = len(members)
    conference = np.zeros((count + 1, count + 1), dtype=np.int64)
    conference[0, 1:] = 1
    conference[1:, 0] = 1
    for row_pos in range(count):
        for col_pos in range(count):
            differ = ((members[row_pos][0] - members[col_pos][0]) % 5, (members[row_pos][1] - members[col_pos][1]) % 5)
            if differ == (0, 0):
                conference[row_pos + 1, col_pos + 1] = 0
            elif differ in squares:
                conference[row_pos + 1, col_pos + 1] = 1
            else:
                conference[row_pos + 1, col_pos + 1] = -1
    plus_block = np.array([[1, 1], [1, -1]], dtype=np.int64)
    zero_block = np.array([[1, -1], [-1, -1]], dtype=np.int64)
    return np.kron(conference, plus_block) + np.kron(np.eye(count + 1, dtype=np.int64), zero_block)


def draw_codes(key, rows_total, cols_total):
    values = jax.random.randint(key, (rows_total, cols_total), -8, 8, dtype=jnp.int32)
    return values.astype(jnp.float32).astype(jnp.bfloat16)


def draw_gate_codes(key, part):
    return draw_codes(jax.random.fold_in(key, 11), D, FF)


def draw_up_codes(key, part):
    return draw_codes(jax.random.fold_in(key, 12), D, FF)


def draw_down_codes(key, part):
    return draw_codes(jax.random.fold_in(key, 13), FF, D)


def draw_hadamard(key, part):
    base = jnp.asarray(paley_table().astype(np.int32))
    row_order = jax.random.permutation(jax.random.fold_in(key, 21), HB)
    col_order = jax.random.permutation(jax.random.fold_in(key, 22), HB)
    row_signs = 2 * jax.random.randint(jax.random.fold_in(key, 23), (HB,), 0, 2, dtype=jnp.int32) - 1
    col_signs = 2 * jax.random.randint(jax.random.fold_in(key, 24), (HB,), 0, 2, dtype=jnp.int32) - 1
    table = base[row_order][:, col_order]
    return (table * row_signs[:, None] * col_signs[None, :]).astype(jnp.int32)


def levels(own_key, extent, pieces, least, top_value):
    loudness = 1.0
    for axis_at, blocks in pieces:
        steps = jax.random.uniform(jax.random.fold_in(jax.random.fold_in(own_key, 6), axis_at), (blocks,), jnp.float32, least / len(pieces), top_value / len(pieces))
        loudness = loudness * jnp.repeat(jnp.exp(steps), extent[axis_at] // blocks).reshape((-1,) + (1,) * (len(extent) - 1 - axis_at))
    return loudness


def gaussian(rng, extent, width, bound, shards=(), kind=jnp.bfloat16):
    result = jax.random.normal(rng, extent, jnp.float32) * width
    if len(shards) > 0:
        result = levels(rng, extent, shards, -0.22, 0.18) * result
    return jnp.clip(result, min=-bound, max=bound).astype(kind)


def setup_inputs(seed: int = 0, part: int = 0) -> dict:
    seeds = jax.random.split(jax.random.key(seed), 9)
    part_splits = jax.random.split(jax.random.fold_in(seeds[8], part), 9)
    tokens = gaussian(part_splits[0], (TOKENS, D), 1.0, 6.0, ((0, 16),))
    gate_codes = draw_gate_codes(jax.random.fold_in(seeds[8], 71), part)
    gate_scales = jnp.clip(jnp.exp(math.log(0.00773398) - 2.3025851 * jax.random.uniform(seeds[2], (D // GROUP, FF), jnp.float32) ** levels(seeds[2], (D // GROUP, FF), ((1, 16),), -0.2, 0.2)), 0.00077339803, 0.00773398)
    up_codes = draw_up_codes(jax.random.fold_in(seeds[8], 71), part)
    up_scales = jnp.clip(jnp.exp(math.log(0.00773398) - 2.3025851 * jax.random.uniform(seeds[4], (D // GROUP, FF), jnp.float32) ** levels(seeds[4], (D // GROUP, FF), ((1, 16),), -0.2, 0.2)), 0.00077339803, 0.00773398)
    down_codes = draw_down_codes(jax.random.fold_in(seeds[8], 71), part)
    down_scales = jnp.clip(jnp.exp(jax.random.uniform(seeds[6], (D,), jnp.float32, math.log(0.00061286293), math.log(0.006128629))), 0.00061286293, 0.006128629)
    hadamard = draw_hadamard(jax.random.fold_in(seeds[8], 71), part)
    return {"tokens": tokens, "gate_codes": gate_codes, "gate_scales": gate_scales, "up_codes": up_codes, "up_scales": up_scales, "down_codes": down_codes, "down_scales": down_scales, "hadamard": hadamard}


def sylvester(size):
    index_vec = jnp.arange(size, dtype=jnp.int32)
    parity = jnp.zeros((size, size), jnp.int32)
    for level in range(max(size.bit_length() - 1, 0)):
        left_bits = jnp.right_shift(index_vec[:, None], level) & 1
        right_bits = jnp.right_shift(index_vec[None, :], level) & 1
        parity = parity + left_bits * right_bits
    return (1 - 2 * (parity % 2)).astype(jnp.float32)

def dequantize(codes, scales):
    row_total, col_total = codes.shape
    group_total = scales.shape[0]
    grouped = codes.astype(jnp.float32).reshape(group_total, row_total // group_total, col_total)
    return (grouped * scales[:, None, :]).reshape(row_total, col_total).astype(jnp.bfloat16)

def reference(tokens, gate_codes, gate_scales, up_codes, up_scales, down_codes, down_scales, hadamard):
    gate_weight = dequantize(gate_codes, gate_scales)
    gate = jnp.dot(tokens, gate_weight, preferred_element_type=jnp.float32)
    up_weight = dequantize(up_codes, up_scales)
    up_part = jnp.dot(tokens, up_weight, preferred_element_type=jnp.float32)
    hidden = jax.nn.silu(gate) * up_part
    cube = hidden.reshape(TOKENS, HA, HB)
    cube = jnp.einsum('tab,ac->tcb', cube, sylvester(HA), precision=lax.Precision.HIGHEST)
    cube = jnp.einsum('tcb,bd->tcd', cube, hadamard.astype(jnp.float32), precision=lax.Precision.HIGHEST)
    rotated = (cube.reshape(TOKENS, FF) * (1.0 / math.sqrt(FF))).astype(jnp.bfloat16)
    summed = jnp.dot(rotated, down_codes, preferred_element_type=jnp.float32)
    return (summed * down_scales[None, :]).astype(jnp.bfloat16)
```

```python
import functools
import math

import jax
import jax.numpy as jnp
from jax import lax
from jax.experimental import pallas as pl
from jax.experimental.pallas import tpu as pltpu
from jax.sharding import PartitionSpec as P

HA = 512
HB = 52
FF = 26624


def sylvester(size):
    index_vec = jnp.arange(size, dtype=jnp.int32)
    parity = jnp.zeros((size, size), jnp.int32)
    for level in range(max(size.bit_length() - 1, 0)):
        left_bits = jnp.right_shift(index_vec[:, None], level) & 1
        right_bits = jnp.right_shift(index_vec[None, :], level) & 1
        parity = parity + left_bits * right_bits
    return (1 - 2 * (parity % 2)).astype(jnp.float32)


def dequantize(codes, scales):
    row_total, col_total = codes.shape
    group_total = scales.shape[0]
    grouped = codes.astype(jnp.float32).reshape(group_total, row_total // group_total, col_total)
    return (grouped * scales[:, None, :]).reshape(row_total, col_total).astype(jnp.bfloat16)


LANES = 128
ROWS = 16
CHUNK_GROUPS = 4
SLOTS = 7


def kernel(
    n, tok_ref, gate_ref, gscale_ref, up_ref, uscale_ref, down_ref, dscale_ref, spread_ref, table_ref,
    out_ref,
    ring, gs, us, down, ds, spread, table, local, tok, stage, lhs, acc, zbuf, recv_z, rbuf, rot, part, sendbuf, recv_c,
    ring_sem, load_sem, down_sem, tok_own, tok_send, tok_recv, z_send, z_recv, r_send, r_recv, c_send, c_recv,
):
    me = lax.axis_index("hx")
    pieces = tok.shape[0]
    units = gate_ref.shape[1]
    owners = units // LANES
    chunk_rows = ring.shape[2]
    chunks = gate_ref.shape[0] // chunk_rows
    down_chunks, _, down_cols = down.shape
    out_pieces = recv_c.shape[0]
    peers = [lax.rem(me + step, n) for step in range(1, n)]

    def gate_copy(c, slot):
        rows = pl.ds(pl.multiple_of(c * chunk_rows, chunk_rows), chunk_rows)
        return pltpu.make_async_copy(gate_ref.at[rows], ring.at[slot, 0], ring_sem.at[slot, 0])

    def up_copy(c, slot):
        rows = pl.ds(pl.multiple_of(c * chunk_rows, chunk_rows), chunk_rows)
        return pltpu.make_async_copy(up_ref.at[rows], ring.at[slot, 1], ring_sem.at[slot, 1])

    def down_copy(c):
        cols = pl.ds(pl.multiple_of(c * down_cols, down_cols), down_cols)
        return pltpu.make_async_copy(down_ref.at[:, cols], down.at[c], down_sem.at[c])

    loads = [
        pltpu.make_async_copy(src, dst, load_sem.at[i])
        for i, (src, dst) in enumerate(
            ((spread_ref, spread), (table_ref, table), (gscale_ref, gs), (uscale_ref, us), (dscale_ref, ds))
        )
    ]
    own_tok = [
        pltpu.make_async_copy(tok_ref.at[pl.ds(p * ROWS, ROWS)], tok.at[p, me], tok_own.at[p])
        for p in range(pieces)
    ]

    barrier = pltpu.get_barrier_semaphore()
    for peer in peers:
        pl.semaphore_signal(barrier, inc=1, device_id={"hx": peer}, device_id_type=pl.DeviceIdType.MESH)
    for copy in own_tok:
        copy.start()
    for copy in loads:
        copy.start()
    for c in range(SLOTS):
        gate_copy(c, c).start()
        up_copy(c, c).start()
    pl.semaphore_wait(barrier, n - 1)

    def remote(src, dst, send_sem, recv_sem, peer):
        return pltpu.make_async_remote_copy(
            src_ref=src, dst_ref=dst, send_sem=send_sem, recv_sem=recv_sem,
            device_id={"hx": peer}, device_id_type=pl.DeviceIdType.MESH,
        )

    def tok_out(p, i):
        return remote(
            tok_ref.at[pl.ds(p * ROWS, ROWS)], tok.at[p, me], tok_send.at[p, i], tok_recv.at[p, me], peers[i]
        )

    def tok_in(p, i):
        return remote(
            tok_ref.at[pl.ds(p * ROWS, ROWS)], tok.at[p, peers[i]], tok_send.at[p, i], tok_recv.at[p, peers[i]],
            peers[i],
        )

    for p in range(pieces):
        for i in range(n - 1):
            tok_out(p, i).start()

    lhs[...] = jnp.zeros_like(lhs)
    acc[...] = jnp.zeros_like(acc)
    for copy in loads:
        copy.wait()

    def build(i, carry):
        rows = pl.ds(pl.multiple_of(i * LANES, LANES), LANES)
        both = jnp.dot(spread[rows, :], table[...], preferred_element_type=jnp.float32)
        local[rows, :] = (both[:, :units] * both[:, units:]).astype(jnp.bfloat16)
        return carry

    lax.fori_loop(0, units // LANES, build, 0)

    pairs_piece = ROWS // 2
    chunks_piece = chunks // pieces
    pairs_chunk = CHUNK_GROUPS // 2
    for p in range(pieces):
        own_tok[p].wait()
        for i in range(n - 1):
            tok_in(p, i).wait_recv()
        stage[...] = tok[p].reshape(n * ROWS, LANES).astype(jnp.float32)
        for q in range(pairs_piece):
            lhs[q, :n, :LANES] = stage[pl.ds(2 * q, n, stride=ROWS), :].astype(jnp.bfloat16)
            lhs[q, n:, LANES:] = stage[pl.ds(2 * q + 1, n, stride=ROWS), :].astype(jnp.bfloat16)

        def step(k, carry):
            c = p * chunks_piece + k
            slot = lax.rem(c, SLOTS)
            gate_copy(c, slot).wait()
            up_copy(c, slot).wait()
            for q in range(pairs_chunk):
                left = lhs[k * pairs_chunk + q]
                row = c * CHUNK_GROUPS + 2 * q
                for w, scale in ((0, gs), (1, us)):
                    res = jnp.dot(
                        left, ring[slot, w, 2 * q * LANES : 2 * (q + 1) * LANES, :],
                        preferred_element_type=jnp.float32,
                    )
                    acc[w] += res[:n] * scale[pl.ds(row, 1), :] + res[n:] * scale[pl.ds(row + 1, 1), :]

            @pl.when(c + SLOTS < chunks)
            def _():
                gate_copy(c + SLOTS, slot).start()
                up_copy(c + SLOTS, slot).start()

            @pl.when(jnp.logical_and(c + SLOTS >= chunks, c + SLOTS - chunks < down_chunks))
            def _():
                down_copy(c + SLOTS - chunks).start()

            return carry

        lax.fori_loop(0, chunks_piece, step, 0)
    for c in range(SLOTS, down_chunks):
        down_copy(c).start()

    gate = acc[0]
    hidden = (gate / (1.0 + jnp.exp(-gate)) * acc[1]).astype(jnp.bfloat16)
    turned = jnp.dot(hidden, local[...], preferred_element_type=jnp.float32).astype(jnp.bfloat16)
    for j in range(owners):
        zbuf[j] = turned[:, j * LANES : (j + 1) * LANES]

    def z_out(j):
        return remote(zbuf.at[j], recv_z.at[me], z_send.at[j], z_recv.at[me], j)

    for j in range(owners):

        @pl.when(me != j)
        def _():
            z_out(j).start()

        @pl.when(me == j)
        def _():
            recv_z[j] = zbuf[j]

    def r_out(i):
        return remote(rbuf.at[peers[i]], rot.at[me], r_send.at[i], r_recv.at[me], peers[i])

    @pl.when(me < owners)
    def _():
        for i in range(n - 1):
            remote(zbuf.at[0], recv_z.at[peers[i]], z_send.at[0], z_recv.at[peers[i]], peers[i]).wait_recv()
        cube = [recv_z[h].astype(jnp.float32) for h in range(n)]
        span = 1
        while span < n:
            nxt = list(cube)
            for h in range(n):
                if h & span == 0:
                    nxt[h] = cube[h] + cube[h | span]
                    nxt[h | span] = cube[h] - cube[h | span]
            cube = nxt
            span *= 2
        for h in range(n):
            rbuf[h] = (cube[h] * (1.0 / math.sqrt(FF))).astype(jnp.bfloat16)
        for i in range(n - 1):
            r_out(i).start()
        rot[me] = rbuf[me]

    for j in range(owners):

        @pl.when(me != j)
        def _():
            remote(rbuf.at[0], rot.at[j], r_send.at[0], r_recv.at[j], j).wait_recv()

    rotated = jnp.concatenate([rot[j] for j in range(owners)], axis=1)

    def c_out(p, i):
        return remote(sendbuf.at[p, peers[i]], recv_c.at[p, me], c_send.at[p, i], c_recv.at[p, me], peers[i])

    def c_in(p, i):
        return remote(
            sendbuf.at[p, peers[i]], recv_c.at[p, peers[i]], c_send.at[p, i], c_recv.at[p, peers[i]], peers[i]
        )

    per_piece = down_chunks // out_pieces
    blocks = down_cols // LANES
    for p in range(out_pieces):
        for k in range(per_piece):
            c = p * per_piece + k
            down_copy(c).wait()
            res = jnp.dot(rotated, down[c], preferred_element_type=jnp.float32)
            for b in range(blocks):
                part[pl.ds(k * blocks + b, n, stride=ROWS), :] = res[:, b * LANES : (b + 1) * LANES]
        sendbuf[p] = part[...].astype(jnp.bfloat16).reshape(n, ROWS, LANES)
        for i in range(n - 1):
            c_out(p, i).start()
        recv_c[p, me] = sendbuf[p, me]

    for p in range(out_pieces):
        for i in range(n - 1):
            c_in(p, i).wait_recv()
        total = recv_c[p, 0].astype(jnp.float32)
        for h in range(1, n):
            total = total + recv_c[p, h].astype(jnp.float32)
        rows = slice(p * ROWS, (p + 1) * ROWS)
        out_ref[rows, :] = (total * ds[rows, :]).astype(out_ref.dtype)

    for p in range(pieces):
        for i in range(n - 1):
            tok_out(p, i).wait_send()
    for j in range(owners):

        @pl.when(me != j)
        def _():
            z_out(j).wait_send()

    @pl.when(me < owners)
    def _():
        for i in range(n - 1):
            r_out(i).wait_send()

    for p in range(out_pieces):
        for i in range(n - 1):
            c_out(p, i).wait_send()


def fused(n, tokens, gate_codes, gate_scales, up_codes, up_scales, down_codes, down_scales, hadamard):
    depth, units = gate_codes.shape
    width = down_codes.shape[1]
    local_a = HA // n
    unit = jnp.arange(units, dtype=jnp.int32)
    lane = jnp.arange(LANES, dtype=jnp.int32)
    half = LANES // 2
    spread = (
        (lane[None, :] == (unit % HB)[:, None]) | (lane[None, :] == half + (unit // HB)[:, None])
    ).astype(jnp.bfloat16)
    small = jnp.tile(hadamard.astype(jnp.bfloat16), (1, local_a))
    signs = jnp.repeat(sylvester(local_a).astype(jnp.bfloat16), HB, axis=1)
    table = jnp.concatenate(
        [
            jnp.pad(small, ((0, half - HB), (0, units))),
            jnp.pad(signs, ((0, half - local_a), (units, 0))),
        ],
        axis=0,
    )
    pieces = depth // (LANES * ROWS)
    out_pieces = width // (LANES * ROWS)
    owners = units // LANES
    chunk_rows = CHUNK_GROUPS * LANES
    down_cols = 8 * LANES
    bf16, f32 = jnp.bfloat16, jnp.float32
    dma = pltpu.SemaphoreType.DMA
    out = pl.pallas_call(
        functools.partial(kernel, n),
        out_shape=jax.ShapeDtypeStruct((width // LANES, LANES), bf16),
        in_specs=[pl.BlockSpec(memory_space=pl.ANY)] * 9,
        out_specs=pl.BlockSpec(memory_space=pltpu.VMEM),
        scratch_shapes=[
            pltpu.VMEM((SLOTS, 2, chunk_rows, units), bf16),
            pltpu.VMEM(gate_scales.shape, f32),
            pltpu.VMEM(up_scales.shape, f32),
            pltpu.VMEM((width // down_cols, units, down_cols), bf16),
            pltpu.VMEM((width // LANES, LANES), f32),
            pltpu.VMEM((units, LANES), bf16),
            pltpu.VMEM((LANES, 2 * units), bf16),
            pltpu.VMEM((units, units), bf16),
            pltpu.VMEM((pieces, n, ROWS, LANES), bf16),
            pltpu.VMEM((n * ROWS, LANES), f32),
            pltpu.VMEM((ROWS // 2, 2 * n, 2 * LANES), bf16),
            pltpu.VMEM((2, n, units), f32),
            pltpu.VMEM((owners, n, LANES), bf16),
            pltpu.VMEM((n, n, LANES), bf16),
            pltpu.VMEM((n, n, LANES), bf16),
            pltpu.VMEM((owners, n, LANES), bf16),
            pltpu.VMEM((n * ROWS, LANES), f32),
            pltpu.VMEM((out_pieces, n, ROWS, LANES), bf16),
            pltpu.VMEM((out_pieces, n, ROWS, LANES), bf16),
            dma((SLOTS, 2)),
            dma((5,)),
            dma((width // down_cols,)),
            dma((pieces,)),
            dma((pieces, n - 1)),
            dma((pieces, n)),
            dma((owners,)),
            dma((n,)),
            dma((n - 1,)),
            dma((owners,)),
            dma((out_pieces, n - 1)),
            dma((out_pieces, n)),
        ],
        compiler_params=pltpu.CompilerParams(
            collective_id=0, has_side_effects=True, vmem_limit_bytes=67043328
        ),
    )(
        tokens.reshape(depth // LANES, LANES), gate_codes, gate_scales, up_codes, up_scales, down_codes,
        down_scales.reshape(width // LANES, LANES), spread, table,
    )
    return out.reshape(1, width)


def fits(n, tokens, gate_codes, gate_scales, down_codes):
    rows, depth = tokens.shape
    units, width = down_codes.shape
    return (
        rows == 1
        and n == ROWS
        and HA % n == 0
        and HA // n <= LANES // 2
        and depth == gate_scales.shape[0] * LANES
        and depth % (ROWS * LANES) == 0
        and width % (ROWS * LANES) == 0
        and units % LANES == 0
        and units // LANES <= n
    )


def per_device(
    tokens, gate_codes, gate_scales, up_codes, up_scales, down_codes, down_scales, hadamard
):
    n = lax.axis_size("hx")
    if fits(n, tokens, gate_codes, gate_scales, down_codes):
        return fused(
            n, tokens, gate_codes, gate_scales, up_codes, up_scales, down_codes, down_scales, hadamard
        )
    gate_weight = dequantize(gate_codes, gate_scales)
    up_weight = dequantize(up_codes, up_scales)
    tile_rows = lax.all_gather(tokens, "hx", axis=0, tiled=True)
    gate = jnp.dot(tile_rows, gate_weight, preferred_element_type=jnp.float32)
    up_part = jnp.dot(tile_rows, up_weight, preferred_element_type=jnp.float32)
    hidden = jax.nn.silu(gate) * up_part
    factor = hadamard.astype(jnp.float32)
    gathered = lax.all_to_all(
        hidden.astype(jnp.bfloat16), "hx", split_axis=0, concat_axis=1, tiled=True
    ).astype(hidden.dtype)
    row_count = gathered.shape[0]
    cube = gathered.reshape(row_count, HA, HB)
    cube = jnp.einsum("tab,ac->tcb", cube, sylvester(HA), precision=lax.Precision.HIGHEST)
    cube = jnp.einsum("tcb,bd->tcd", cube, factor, precision=lax.Precision.HIGHEST)
    turned = lax.all_to_all(
        cube.reshape(row_count, FF).astype(jnp.bfloat16),
        "hx",
        split_axis=1,
        concat_axis=0,
        tiled=True,
    ).astype(jnp.float32)
    rotated = (turned * (1.0 / math.sqrt(FF))).astype(jnp.bfloat16)
    summed = lax.psum_scatter(
        jnp.dot(rotated, down_codes, preferred_element_type=jnp.float32),
        "hx",
        scatter_dimension=0,
        tiled=True,
    )
    mixed = (summed * down_scales[None, :]).astype(jnp.bfloat16)
    return mixed


def solution(mesh):
    in_specs = (
        P(("groups", "hx"), None),
        P(None, "hx"),
        P(None, "hx"),
        P(None, "hx"),
        P(None, "hx"),
        P("hx", None),
        P(),
        P(),
    )
    out_specs = P(("groups", "hx"), None)
    return jax.shard_map(
        per_device, mesh=mesh, in_specs=in_specs, out_specs=out_specs, check_vma=False
    )
```

```python
import functools
import math

import jax
import jax.numpy as jnp
from jax import lax
from jax.experimental import pallas as pl
from jax.experimental.pallas import tpu as pltpu
from jax.sharding import PartitionSpec as P

HA = 512
HB = 52
FF = 26624


def sylvester(size):
    index_vec = jnp.arange(size, dtype=jnp.int32)
    parity = jnp.zeros((size, size), jnp.int32)
    for level in range(max(size.bit_length() - 1, 0)):
        left_bits = jnp.right_shift(index_vec[:, None], level) & 1
        right_bits = jnp.right_shift(index_vec[None, :], level) & 1
        parity = parity + left_bits * right_bits
    return (1 - 2 * (parity % 2)).astype(jnp.float32)


def dequantize(codes, scales):
    row_total, col_total = codes.shape
    group_total = scales.shape[0]
    grouped = codes.astype(jnp.float32).reshape(group_total, row_total // group_total, col_total)
    return (grouped * scales[:, None, :]).reshape(row_total, col_total).astype(jnp.bfloat16)


LANES = 128
ROWS = 16
CHUNK_GROUPS = 4
SLOTS = 7


def kernel(
    n, tok_ref, gate_ref, gscale_ref, up_ref, uscale_ref, down_ref, dscale_ref, had_ref,
    out_ref,
    ring, gs, us, down, ds, had, corner, table, local, tok_row, tok_f32, tok_out_buf, tok, stage, lhs, acc, zbuf, recv_z, rbuf, rot, part, sendbuf, recv_c,
    ring_sem, load_sem, down_sem, tok_send, tok_recv, z_send, z_recv, r_send, r_recv, c_send, c_recv,
):
    me = lax.axis_index("hx")
    pieces = tok.shape[0]
    units = gate_ref.shape[1]
    owners = units // LANES
    chunk_rows = ring.shape[2]
    chunks = gate_ref.shape[0] // chunk_rows
    down_chunks, _, down_cols = down.shape
    out_pieces = recv_c.shape[0]
    peers = [lax.rem(me + step, n) for step in range(1, n)]

    def gate_copy(c, slot):
        rows = pl.ds(pl.multiple_of(c * chunk_rows, chunk_rows), chunk_rows)
        return pltpu.make_async_copy(gate_ref.at[rows], ring.at[slot, 0], ring_sem.at[slot, 0])

    def up_copy(c, slot):
        rows = pl.ds(pl.multiple_of(c * chunk_rows, chunk_rows), chunk_rows)
        return pltpu.make_async_copy(up_ref.at[rows], ring.at[slot, 1], ring_sem.at[slot, 1])

    def down_copy(c):
        cols = pl.ds(pl.multiple_of(c * down_cols, down_cols), down_cols)
        return pltpu.make_async_copy(down_ref.at[:, cols], down.at[c], down_sem.at[c])

    loads = [
        pltpu.make_async_copy(src, dst, load_sem.at[i])
        for i, (src, dst) in enumerate(
            ((tok_ref, tok_row), (had_ref, had), (dscale_ref, ds), (gscale_ref, gs), (uscale_ref, us))
        )
    ]

    barrier = pltpu.get_barrier_semaphore()
    for peer in peers:
        pl.semaphore_signal(barrier, inc=1, device_id={"hx": peer}, device_id_type=pl.DeviceIdType.MESH)
    for copy in loads:
        copy.start()
    for c in range(SLOTS):
        gate_copy(c, c).start()
        up_copy(c, c).start()
    loads[0].wait()
    row = tok_row[...].astype(jnp.float32)
    for k in range(pieces * ROWS):
        tok_f32[k : k + 1, :] = row[:, k * LANES : (k + 1) * LANES]
    tok_out_buf[...] = tok_f32[...].astype(jnp.bfloat16)
    for p in range(pieces):
        tok[p, me] = tok_out_buf[p * ROWS : (p + 1) * ROWS, :]
    pl.semaphore_wait(barrier, n - 1)

    def remote(src, dst, send_sem, recv_sem, peer):
        return pltpu.make_async_remote_copy(
            src_ref=src, dst_ref=dst, send_sem=send_sem, recv_sem=recv_sem,
            device_id={"hx": peer}, device_id_type=pl.DeviceIdType.MESH,
        )

    def tok_out(p, i):
        return remote(
            tok_out_buf.at[pl.ds(p * ROWS, ROWS)], tok.at[p, me], tok_send.at[p, i], tok_recv.at[p, me], peers[i]
        )

    def tok_in(p, i):
        return remote(
            tok_out_buf.at[pl.ds(p * ROWS, ROWS)], tok.at[p, peers[i]], tok_send.at[p, i], tok_recv.at[p, peers[i]],
            peers[i],
        )

    for p in range(pieces):
        for i in range(n - 1):
            tok_out(p, i).start()

    lhs[...] = jnp.zeros_like(lhs)
    acc[...] = jnp.zeros_like(acc)
    for copy in loads[1:]:
        copy.wait()

    half = LANES // 2
    hb = had.shape[0]
    ha = units // hb
    corner[...] = jnp.zeros_like(corner)
    corner[:hb, :hb] = had[...].astype(jnp.float32)
    left_bits = lax.broadcasted_iota(jnp.int32, (ha, ha), 0) & lax.broadcasted_iota(jnp.int32, (ha, ha), 1)
    parity = jnp.zeros((ha, ha), jnp.int32)
    for level in range(ha.bit_length() - 1):
        parity = parity ^ (jnp.right_shift(left_bits, level) & 1)
    corner[half : half + ha, half : half + ha] = (1 - 2 * parity).astype(jnp.float32)

    def digits(unit):
        high = jnp.floor((unit + 0.5) * (1.0 / hb))
        return high, unit - hb * high

    def wide(i, carry):
        shape = (LANES, LANES)
        unit = (lax.broadcasted_iota(jnp.int32, shape, 1) + i * LANES).astype(jnp.float32)
        at = lax.broadcasted_iota(jnp.int32, shape, 0).astype(jnp.float32)
        high, low = digits(unit)
        pick = jnp.where((at == low) | (at == high + half), 1.0, 0.0).astype(jnp.bfloat16)
        table[i] = jnp.dot(
            corner[...].astype(jnp.bfloat16), pick, preferred_element_type=jnp.float32
        ).astype(jnp.bfloat16)
        return carry

    lax.fori_loop(0, owners, wide, 0)
    factors = jnp.concatenate([table[j] for j in range(owners)], axis=1)

    def build(i, carry):
        shape = (LANES, LANES)
        unit = (lax.broadcasted_iota(jnp.int32, shape, 0) + i * LANES).astype(jnp.float32)
        at = lax.broadcasted_iota(jnp.int32, shape, 1).astype(jnp.float32)
        high, low = digits(unit)
        pick = jnp.concatenate(
            [jnp.where(at == low, 1.0, 0.0), jnp.where(at == high + half, 1.0, 0.0)], axis=0
        ).astype(jnp.bfloat16)
        both = jnp.dot(pick, factors, preferred_element_type=jnp.float32)
        rows = pl.ds(pl.multiple_of(i * LANES, LANES), LANES)
        local[rows, :] = (both[:LANES] * both[LANES:]).astype(jnp.bfloat16)
        return carry

    lax.fori_loop(0, units // LANES, build, 0)

    pairs_piece = ROWS // 2
    chunks_piece = chunks // pieces
    pairs_chunk = CHUNK_GROUPS // 2
    for p in range(pieces):
        for i in range(n - 1):
            tok_in(p, i).wait_recv()
        stage[...] = tok[p].reshape(n * ROWS, LANES).astype(jnp.float32)
        for q in range(pairs_piece):
            lhs[q, :n, :LANES] = stage[pl.ds(2 * q, n, stride=ROWS), :].astype(jnp.bfloat16)
            lhs[q, n:, LANES:] = stage[pl.ds(2 * q + 1, n, stride=ROWS), :].astype(jnp.bfloat16)

        def step(k, carry):
            c = p * chunks_piece + k
            slot = lax.rem(c, SLOTS)
            gate_copy(c, slot).wait()
            up_copy(c, slot).wait()
            for q in range(pairs_chunk):
                left = lhs[k * pairs_chunk + q]
                row = c * CHUNK_GROUPS + 2 * q
                for w, scale in ((0, gs), (1, us)):
                    res = jnp.dot(
                        left, ring[slot, w, 2 * q * LANES : 2 * (q + 1) * LANES, :],
                        preferred_element_type=jnp.float32,
                    )
                    acc[w] += res[:n] * scale[pl.ds(row, 1), :] + res[n:] * scale[pl.ds(row + 1, 1), :]

            @pl.when(c + SLOTS < chunks)
            def _():
                gate_copy(c + SLOTS, slot).start()
                up_copy(c + SLOTS, slot).start()

            @pl.when(jnp.logical_and(c + SLOTS >= chunks, c + SLOTS - chunks < down_chunks))
            def _():
                down_copy(c + SLOTS - chunks).start()

            return carry

        lax.fori_loop(0, chunks_piece, step, 0)
    for c in range(SLOTS, down_chunks):
        down_copy(c).start()

    gate = acc[0]
    hidden = (gate / (1.0 + jnp.exp(-gate)) * acc[1]).astype(jnp.bfloat16)
    turned = jnp.dot(hidden, local[...], preferred_element_type=jnp.float32).astype(jnp.bfloat16)
    for j in range(owners):
        zbuf[j] = turned[:, j * LANES : (j + 1) * LANES]

    def z_out(j):
        return remote(zbuf.at[j], recv_z.at[me], z_send.at[j], z_recv.at[me], j)

    for j in range(owners):

        @pl.when(me != j)
        def _():
            z_out(j).start()

        @pl.when(me == j)
        def _():
            recv_z[j] = zbuf[j]

    def r_out(i):
        return remote(rbuf.at[peers[i]], rot.at[me], r_send.at[i], r_recv.at[me], peers[i])

    @pl.when(me < owners)
    def _():
        for i in range(n - 1):
            remote(zbuf.at[0], recv_z.at[peers[i]], z_send.at[0], z_recv.at[peers[i]], peers[i]).wait_recv()
        cube = [recv_z[h].astype(jnp.float32) for h in range(n)]
        span = 1
        while span < n:
            nxt = list(cube)
            for h in range(n):
                if h & span == 0:
                    nxt[h] = cube[h] + cube[h | span]
                    nxt[h | span] = cube[h] - cube[h | span]
            cube = nxt
            span *= 2
        for h in range(n):
            rbuf[h] = (cube[h] * (1.0 / math.sqrt(FF))).astype(jnp.bfloat16)
        for i in range(n - 1):
            r_out(i).start()
        rot[me] = rbuf[me]

    for j in range(owners):

        @pl.when(me != j)
        def _():
            remote(rbuf.at[0], rot.at[j], r_send.at[0], r_recv.at[j], j).wait_recv()

    rotated = jnp.concatenate([rot[j] for j in range(owners)], axis=1)

    def c_out(p, i):
        return remote(sendbuf.at[p, peers[i]], recv_c.at[p, me], c_send.at[p, i], c_recv.at[p, me], peers[i])

    def c_in(p, i):
        return remote(
            sendbuf.at[p, peers[i]], recv_c.at[p, peers[i]], c_send.at[p, i], c_recv.at[p, peers[i]], peers[i]
        )

    per_piece = down_chunks // out_pieces
    blocks = down_cols // LANES
    for p in range(out_pieces):
        for k in range(per_piece):
            c = p * per_piece + k
            down_copy(c).wait()
            res = jnp.dot(rotated, down[c], preferred_element_type=jnp.float32)
            for b in range(blocks):
                part[pl.ds(k * blocks + b, n, stride=ROWS), :] = res[:, b * LANES : (b + 1) * LANES]
        sendbuf[p] = part[...].astype(jnp.bfloat16).reshape(n, ROWS, LANES)
        for i in range(n - 1):
            c_out(p, i).start()
        recv_c[p, me] = sendbuf[p, me]

    for p in range(out_pieces):
        for i in range(n - 1):
            c_in(p, i).wait_recv()
        total = recv_c[p, 0].astype(jnp.float32)
        for h in range(1, n):
            total = total + recv_c[p, h].astype(jnp.float32)
        for r in range(ROWS):
            cols = slice((p * ROWS + r) * LANES, (p * ROWS + r + 1) * LANES)
            out_ref[:, cols] = (total[r : r + 1, :] * ds[:, cols]).astype(out_ref.dtype)

    for p in range(pieces):
        for i in range(n - 1):
            tok_out(p, i).wait_send()
    for j in range(owners):

        @pl.when(me != j)
        def _():
            z_out(j).wait_send()

    @pl.when(me < owners)
    def _():
        for i in range(n - 1):
            r_out(i).wait_send()

    for p in range(out_pieces):
        for i in range(n - 1):
            c_out(p, i).wait_send()


def fused(n, tokens, gate_codes, gate_scales, up_codes, up_scales, down_codes, down_scales, hadamard):
    depth, units = gate_codes.shape
    width = down_codes.shape[1]
    pieces = depth // (LANES * ROWS)
    out_pieces = width // (LANES * ROWS)
    owners = units // LANES
    chunk_rows = CHUNK_GROUPS * LANES
    down_cols = 8 * LANES
    bf16, f32 = jnp.bfloat16, jnp.float32
    dma = pltpu.SemaphoreType.DMA
    out = pl.pallas_call(
        functools.partial(kernel, n),
        out_shape=jax.ShapeDtypeStruct((1, width), bf16),
        in_specs=[pl.BlockSpec(memory_space=pl.ANY)] * 8,
        out_specs=pl.BlockSpec(memory_space=pltpu.VMEM),
        scratch_shapes=[
            pltpu.VMEM((SLOTS, 2, chunk_rows, units), bf16),
            pltpu.VMEM(gate_scales.shape, f32),
            pltpu.VMEM(up_scales.shape, f32),
            pltpu.VMEM((width // down_cols, units, down_cols), bf16),
            pltpu.VMEM((1, width), f32),
            pltpu.VMEM(hadamard.shape, hadamard.dtype),
            pltpu.VMEM((LANES, LANES), f32),
            pltpu.VMEM((owners, LANES, LANES), bf16),
            pltpu.VMEM((units, units), bf16),
            pltpu.VMEM((1, depth), bf16),
            pltpu.VMEM((depth // LANES, LANES), f32),
            pltpu.VMEM((depth // LANES, LANES), bf16),
            pltpu.VMEM((pieces, n, ROWS, LANES), bf16),
            pltpu.VMEM((n * ROWS, LANES), f32),
            pltpu.VMEM((ROWS // 2, 2 * n, 2 * LANES), bf16),
            pltpu.VMEM((2, n, units), f32),
            pltpu.VMEM((owners, n, LANES), bf16),
            pltpu.VMEM((n, n, LANES), bf16),
            pltpu.VMEM((n, n, LANES), bf16),
            pltpu.VMEM((owners, n, LANES), bf16),
            pltpu.VMEM((n * ROWS, LANES), f32),
            pltpu.VMEM((out_pieces, n, ROWS, LANES), bf16),
            pltpu.VMEM((out_pieces, n, ROWS, LANES), bf16),
            dma((SLOTS, 2)),
            dma((5,)),
            dma((width // down_cols,)),
            dma((pieces, n - 1)),
            dma((pieces, n)),
            dma((owners,)),
            dma((n,)),
            dma((n - 1,)),
            dma((owners,)),
            dma((out_pieces, n - 1)),
            dma((out_pieces, n)),
        ],
        compiler_params=pltpu.CompilerParams(
            collective_id=0, has_side_effects=True, vmem_limit_bytes=67043328
        ),
    )(
        tokens, gate_codes, gate_scales, up_codes, up_scales, down_codes, down_scales.reshape(1, width), hadamard,
    )
    return out


def fits(n, tokens, gate_codes, gate_scales, down_codes):
    rows, depth = tokens.shape
    units, width = down_codes.shape
    return (
        rows == 1
        and n == ROWS
        and HA % n == 0
        and HA // n <= LANES // 2
        and HB <= LANES // 2
        and depth == gate_scales.shape[0] * LANES
        and depth % (ROWS * LANES) == 0
        and width % (ROWS * LANES) == 0
        and units % LANES == 0
        and units // LANES <= n
    )


def per_device(
    tokens, gate_codes, gate_scales, up_codes, up_scales, down_codes, down_scales, hadamard
):
    n = lax.axis_size("hx")
    if fits(n, tokens, gate_codes, gate_scales, down_codes):
        return fused(
            n, tokens, gate_codes, gate_scales, up_codes, up_scales, down_codes, down_scales, hadamard
        )
    gate_weight = dequantize(gate_codes, gate_scales)
    up_weight = dequantize(up_codes, up_scales)
    tile_rows = lax.all_gather(tokens, "hx", axis=0, tiled=True)
    gate = jnp.dot(tile_rows, gate_weight, preferred_element_type=jnp.float32)
    up_part = jnp.dot(tile_rows, up_weight, preferred_element_type=jnp.float32)
    hidden = jax.nn.silu(gate) * up_part
    factor = hadamard.astype(jnp.float32)
    gathered = lax.all_to_all(
        hidden.astype(jnp.bfloat16), "hx", split_axis=0, concat_axis=1, tiled=True
    ).astype(hidden.dtype)
    row_count = gathered.shape[0]
    cube = gathered.reshape(row_count, HA, HB)
    cube = jnp.einsum("tab,ac->tcb", cube, sylvester(HA), precision=lax.Precision.HIGHEST)
    cube = jnp.einsum("tcb,bd->tcd", cube, factor, precision=lax.Precision.HIGHEST)
    turned = lax.all_to_all(
        cube.reshape(row_count, FF).astype(jnp.bfloat16),
        "hx",
        split_axis=1,
        concat_axis=0,
        tiled=True,
    ).astype(jnp.float32)
    rotated = (turned * (1.0 / math.sqrt(FF))).astype(jnp.bfloat16)
    summed = lax.psum_scatter(
        jnp.dot(rotated, down_codes, preferred_element_type=jnp.float32),
        "hx",
        scatter_dimension=0,
        tiled=True,
    )
    mixed = (summed * down_scales[None, :]).astype(jnp.bfloat16)
    return mixed


def solution(mesh):
    in_specs = (
        P(("groups", "hx"), None),
        P(None, "hx"),
        P(None, "hx"),
        P(None, "hx"),
        P(None, "hx"),
        P("hx", None),
        P(),
        P(),
    )
    out_specs = P(("groups", "hx"), None)
    return jax.shard_map(
        per_device, mesh=mesh, in_specs=in_specs, out_specs=out_specs, check_vma=False
    )
```

```python
import functools
import math

import jax
import jax.numpy as jnp
from jax import lax
from jax.experimental import pallas as pl
from jax.experimental.pallas import tpu as pltpu
from jax.sharding import PartitionSpec as P

HA = 512
HB = 52
FF = 26624


def sylvester(size):
    index_vec = jnp.arange(size, dtype=jnp.int32)
    parity = jnp.zeros((size, size), jnp.int32)
    for level in range(max(size.bit_length() - 1, 0)):
        left_bits = jnp.right_shift(index_vec[:, None], level) & 1
        right_bits = jnp.right_shift(index_vec[None, :], level) & 1
        parity = parity + left_bits * right_bits
    return (1 - 2 * (parity % 2)).astype(jnp.float32)


def dequantize(codes, scales):
    row_total, col_total = codes.shape
    group_total = scales.shape[0]
    grouped = codes.astype(jnp.float32).reshape(group_total, row_total // group_total, col_total)
    return (grouped * scales[:, None, :]).reshape(row_total, col_total).astype(jnp.bfloat16)


LANES = 128
ROWS = 16
CHUNK_GROUPS = 4


def kernel(
    n, parts, tok_ref, gate_ref, gscale_ref, up_ref, uscale_ref, down_ref, dscale_ref, had_ref,
    out_ref,
    ring, gs, us, down, ds, had, corner, table, local, tok_row, tok_f32, tok_out_buf, tok, stage, lhs, acc, zbuf, recv_z, rbuf, rot, part, sendbuf, recv_c, swap_out, swap_in,
    ring_sem, load_sem, down_sem, tok_send, tok_recv, z_send, z_recv, r_send, r_recv, c_send, c_recv, swap_send, swap_recv,
):
    me = lax.axis_index("hx")
    pieces = tok.shape[0]
    units = gate_ref.shape[1]
    owners = units // LANES
    chunk_rows = ring.shape[2]
    chunks = ring.shape[0]
    mine = lax.axis_index("groups")
    me_all = mine * n + me
    total_n = parts * n
    half_groups = gs.shape[0]
    down_chunks, _, down_cols = down.shape
    out_pieces = recv_c.shape[0]
    peers = [lax.rem(me + step, n) for step in range(1, n)]
    everyone = [lax.rem(me_all + step, total_n) for step in range(1, total_n)]
    sides = [lax.div(peer, n) for peer in everyone]
    spots = [lax.rem(peer, n) for peer in everyone]

    def gate_copy(c, slot):
        rows = pl.ds(pl.multiple_of((mine * chunks + c) * chunk_rows, chunk_rows), chunk_rows)
        return pltpu.make_async_copy(gate_ref.at[rows], ring.at[slot, 0], ring_sem.at[slot, 0])

    def up_copy(c, slot):
        rows = pl.ds(pl.multiple_of((mine * chunks + c) * chunk_rows, chunk_rows), chunk_rows)
        return pltpu.make_async_copy(up_ref.at[rows], ring.at[slot, 1], ring_sem.at[slot, 1])

    def down_copy(c):
        cols = pl.ds(pl.multiple_of((mine * down_chunks + c) * down_cols, down_cols), down_cols)
        return pltpu.make_async_copy(down_ref.at[:, cols], down.at[c], down_sem.at[c])

    loads = [
        pltpu.make_async_copy(src, dst, load_sem.at[i])
        for i, (src, dst) in enumerate(
            (
                (tok_ref, tok_row),
                (had_ref, had),
                (dscale_ref, ds),
                (gscale_ref.at[pl.ds(pl.multiple_of(mine * half_groups, 8), half_groups)], gs),
                (uscale_ref.at[pl.ds(pl.multiple_of(mine * half_groups, 8), half_groups)], us),
            )
        )
    ]

    barrier = pltpu.get_barrier_semaphore()
    for side, spot in zip(sides, spots):
        pl.semaphore_signal(
            barrier, inc=1, device_id={"groups": side, "hx": spot}, device_id_type=pl.DeviceIdType.MESH
        )
    for copy in loads:
        copy.start()
    for c in range(chunks):
        gate_copy(c, c).start()
        up_copy(c, c).start()
    for c in range(down_chunks):
        down_copy(c).start()
    loads[0].wait()
    row = tok_row[...].astype(jnp.float32)
    for k in range(parts * pieces * ROWS):
        tok_f32[k : k + 1, :] = row[:, k * LANES : (k + 1) * LANES]
    tok_out_buf[...] = tok_f32[...].astype(jnp.bfloat16)
    for p in range(pieces):
        tok[p, me_all] = tok_out_buf[pl.ds(pl.multiple_of((mine * pieces + p) * ROWS, ROWS), ROWS), :]
    pl.semaphore_wait(barrier, total_n - 1)

    def remote(src, dst, send_sem, recv_sem, peer, side=None):
        side = mine if side is None else side
        return pltpu.make_async_remote_copy(
            src_ref=src, dst_ref=dst, send_sem=send_sem, recv_sem=recv_sem,
            device_id={"groups": side, "hx": peer}, device_id_type=pl.DeviceIdType.MESH,
        )

    def tok_copy(p, i, slot):
        rows = pl.ds(pl.multiple_of((sides[i] * pieces + p) * ROWS, ROWS), ROWS)
        return remote(
            tok_out_buf.at[rows], tok.at[p, slot], tok_send.at[p, i], tok_recv.at[p, slot], spots[i], sides[i]
        )

    for p in range(pieces):
        for i in range(total_n - 1):
            tok_copy(p, i, me_all).start()

    lhs[...] = jnp.zeros_like(lhs)
    acc[...] = jnp.zeros_like(acc)
    for copy in loads[1:]:
        copy.wait()

    half = LANES // 2
    hb = had.shape[0]
    ha = units // hb
    corner[...] = jnp.zeros_like(corner)
    corner[:hb, :hb] = had[...].astype(jnp.float32)
    left_bits = lax.broadcasted_iota(jnp.int32, (ha, ha), 0) & lax.broadcasted_iota(jnp.int32, (ha, ha), 1)
    parity = jnp.zeros((ha, ha), jnp.int32)
    for level in range(ha.bit_length() - 1):
        parity = parity ^ (jnp.right_shift(left_bits, level) & 1)
    corner[half : half + ha, half : half + ha] = (1 - 2 * parity).astype(jnp.float32)

    def digits(unit):
        high = jnp.floor((unit + 0.5) * (1.0 / hb))
        return high, unit - hb * high

    def wide(i, carry):
        shape = (LANES, LANES)
        unit = (lax.broadcasted_iota(jnp.int32, shape, 1) + i * LANES).astype(jnp.float32)
        at = lax.broadcasted_iota(jnp.int32, shape, 0).astype(jnp.float32)
        high, low = digits(unit)
        pick = jnp.where((at == low) | (at == high + half), 1.0, 0.0).astype(jnp.bfloat16)
        table[i] = jnp.dot(
            corner[...].astype(jnp.bfloat16), pick, preferred_element_type=jnp.float32
        ).astype(jnp.bfloat16)
        return carry

    lax.fori_loop(0, owners, wide, 0)
    factors = jnp.concatenate([table[j] for j in range(owners)], axis=1)

    def build(i, carry):
        shape = (LANES, LANES)
        unit = (lax.broadcasted_iota(jnp.int32, shape, 0) + i * LANES).astype(jnp.float32)
        at = lax.broadcasted_iota(jnp.int32, shape, 1).astype(jnp.float32)
        high, low = digits(unit)
        pick = jnp.concatenate(
            [jnp.where(at == low, 1.0, 0.0), jnp.where(at == high + half, 1.0, 0.0)], axis=0
        ).astype(jnp.bfloat16)
        both = jnp.dot(pick, factors, preferred_element_type=jnp.float32)
        rows = pl.ds(pl.multiple_of(i * LANES, LANES), LANES)
        local[rows, :] = (both[:LANES] * both[LANES:]).astype(jnp.bfloat16)
        return carry

    lax.fori_loop(0, units // LANES, build, 0)

    pairs_piece = ROWS // 2
    chunks_piece = chunks // pieces
    pairs_chunk = CHUNK_GROUPS // 2
    for p in range(pieces):
        for i in range(total_n - 1):
            tok_copy(p, i, everyone[i]).wait_recv()
        stage[...] = tok[p].reshape(total_n * ROWS, LANES).astype(jnp.float32)
        for q in range(pairs_piece):
            lhs[q, :total_n, :LANES] = stage[pl.ds(2 * q, total_n, stride=ROWS), :].astype(jnp.bfloat16)
            lhs[q, total_n:, LANES:] = stage[pl.ds(2 * q + 1, total_n, stride=ROWS), :].astype(jnp.bfloat16)

        def step(k, carry):
            c = p * chunks_piece + k
            slot = c
            gate_copy(c, slot).wait()
            up_copy(c, slot).wait()
            for q in range(pairs_chunk):
                left = lhs[k * pairs_chunk + q]
                row = c * CHUNK_GROUPS + 2 * q
                for w, scale in ((0, gs), (1, us)):
                    res = jnp.dot(
                        left, ring[slot, w, 2 * q * LANES : 2 * (q + 1) * LANES, :],
                        preferred_element_type=jnp.float32,
                    )
                    acc[w] += res[:total_n] * scale[pl.ds(row, 1), :] + res[total_n:] * scale[pl.ds(row + 1, 1), :]

            return carry

        lax.fori_loop(0, chunks_piece, step, 0)
    theirs = parts - 1 - mine
    for w in range(2):
        swap_out[w] = acc[w, pl.ds(pl.multiple_of(theirs * n, n), n), :].astype(jnp.bfloat16)
    swap = remote(swap_out, swap_in, swap_send, swap_recv, me, theirs)
    swap.start()
    own = pl.ds(pl.multiple_of(mine * n, n), n)
    swap.wait_recv()
    gate = acc[0, own, :] + swap_in[0].astype(jnp.float32)
    up_part = acc[1, own, :] + swap_in[1].astype(jnp.float32)
    hidden = (gate / (1.0 + jnp.exp(-gate)) * up_part).astype(jnp.bfloat16)
    turned = jnp.dot(hidden, local[...], preferred_element_type=jnp.float32).astype(jnp.bfloat16)
    for j in range(owners):
        zbuf[j] = turned[:, j * LANES : (j + 1) * LANES]

    def z_out(j):
        return remote(zbuf.at[j], recv_z.at[me], z_send.at[j], z_recv.at[me], j)

    for j in range(owners):

        @pl.when(me != j)
        def _():
            z_out(j).start()

        @pl.when(me == j)
        def _():
            recv_z[j] = zbuf[j]

    def r_out(i):
        return remote(
            rbuf.at[spots[i]], rot.at[mine, me], r_send.at[i], r_recv.at[mine, me], spots[i], sides[i]
        )

    @pl.when(me < owners)
    def _():
        for i in range(n - 1):
            remote(zbuf.at[0], recv_z.at[peers[i]], z_send.at[0], z_recv.at[peers[i]], peers[i]).wait_recv()
        cube = [recv_z[h].astype(jnp.float32) for h in range(n)]
        span = 1
        while span < n:
            nxt = list(cube)
            for h in range(n):
                if h & span == 0:
                    nxt[h] = cube[h] + cube[h | span]
                    nxt[h | span] = cube[h] - cube[h | span]
            cube = nxt
            span *= 2
        for h in range(n):
            rbuf[h] = (cube[h] * (1.0 / math.sqrt(FF))).astype(jnp.bfloat16)
        for i in range(total_n - 1):
            r_out(i).start()
        rot[mine, me] = rbuf[me]

    for j in range(owners):
        for side in range(parts):

            @pl.when(jnp.logical_or(me != j, mine != side))
            def _():
                remote(rbuf.at[0], rot.at[side, j], r_send.at[0], r_recv.at[side, j], j, theirs).wait_recv()

    rotated = jnp.concatenate(
        [jnp.concatenate([rot[side, j] for j in range(owners)], axis=1) for side in range(parts)], axis=0
    )

    def c_copy(p, i, slot):
        return remote(
            sendbuf.at[p, everyone[i]], recv_c.at[p, slot], c_send.at[p, i], c_recv.at[p, slot], spots[i], sides[i]
        )

    per_piece = down_chunks // out_pieces
    blocks = down_cols // LANES
    for p in range(out_pieces):
        for k in range(per_piece):
            c = p * per_piece + k
            down_copy(c).wait()
            res = jnp.dot(rotated, down[c], preferred_element_type=jnp.float32)
            for b in range(blocks):
                part[pl.ds(k * blocks + b, total_n, stride=ROWS), :] = res[:, b * LANES : (b + 1) * LANES]
        sendbuf[p] = part[...].astype(jnp.bfloat16).reshape(total_n, ROWS, LANES)
        for i in range(total_n - 1):
            c_copy(p, i, me_all).start()
        recv_c[p, me_all] = sendbuf[p, me_all]

    for p in range(out_pieces):
        for i in range(total_n - 1):
            c_copy(p, i, everyone[i]).wait_recv()
        for side in range(parts):
            total = recv_c[p, side * n].astype(jnp.float32)
            for h in range(1, n):
                total = total + recv_c[p, side * n + h].astype(jnp.float32)
            for r in range(ROWS):
                at = ((side * out_pieces + p) * ROWS + r) * LANES
                cols = slice(at, at + LANES)
                out_ref[:, cols] = (total[r : r + 1, :] * ds[:, cols]).astype(out_ref.dtype)

    swap.wait_send()
    for p in range(pieces):
        for i in range(total_n - 1):
            tok_copy(p, i, me_all).wait_send()
    for j in range(owners):

        @pl.when(me != j)
        def _():
            z_out(j).wait_send()

    @pl.when(me < owners)
    def _():
        for i in range(total_n - 1):
            r_out(i).wait_send()

    for p in range(out_pieces):
        for i in range(total_n - 1):
            c_copy(p, i, me_all).wait_send()


def fused(n, parts, tokens, gate_codes, gate_scales, up_codes, up_scales, down_codes, down_scales, hadamard):
    depth, units = gate_codes.shape
    width = down_codes.shape[1]
    pieces = depth // (LANES * ROWS * parts)
    out_pieces = width // (LANES * ROWS * parts)
    total_n = parts * n
    owners = units // LANES
    chunk_rows = CHUNK_GROUPS * LANES
    down_cols = 8 * LANES
    bf16, f32 = jnp.bfloat16, jnp.float32
    dma = pltpu.SemaphoreType.DMA
    out = pl.pallas_call(
        functools.partial(kernel, n, parts),
        out_shape=jax.ShapeDtypeStruct((1, width), bf16),
        in_specs=[pl.BlockSpec(memory_space=pl.ANY)] * 8,
        out_specs=pl.BlockSpec(memory_space=pltpu.VMEM),
        scratch_shapes=[
            pltpu.VMEM((depth // parts // chunk_rows, 2, chunk_rows, units), bf16),
            pltpu.VMEM((gate_scales.shape[0] // parts, units), f32),
            pltpu.VMEM((up_scales.shape[0] // parts, units), f32),
            pltpu.VMEM((width // parts // down_cols, units, down_cols), bf16),
            pltpu.VMEM((1, width), f32),
            pltpu.VMEM(hadamard.shape, hadamard.dtype),
            pltpu.VMEM((LANES, LANES), f32),
            pltpu.VMEM((owners, LANES, LANES), bf16),
            pltpu.VMEM((units, units), bf16),
            pltpu.VMEM((1, depth), bf16),
            pltpu.VMEM((depth // LANES, LANES), f32),
            pltpu.VMEM((depth // LANES, LANES), bf16),
            pltpu.VMEM((pieces, total_n, ROWS, LANES), bf16),
            pltpu.VMEM((total_n * ROWS, LANES), f32),
            pltpu.VMEM((ROWS // 2, 2 * total_n, 2 * LANES), bf16),
            pltpu.VMEM((2, total_n, units), f32),
            pltpu.VMEM((owners, n, LANES), bf16),
            pltpu.VMEM((n, n, LANES), bf16),
            pltpu.VMEM((n, n, LANES), bf16),
            pltpu.VMEM((parts, owners, n, LANES), bf16),
            pltpu.VMEM((total_n * ROWS, LANES), f32),
            pltpu.VMEM((out_pieces, total_n, ROWS, LANES), bf16),
            pltpu.VMEM((out_pieces, total_n, ROWS, LANES), bf16),
            pltpu.VMEM((2, n, units), bf16),
            pltpu.VMEM((2, n, units), bf16),
            dma((depth // parts // chunk_rows, 2)),
            dma((5,)),
            dma((width // parts // down_cols,)),
            dma((pieces, total_n - 1)),
            dma((pieces, total_n)),
            dma((owners,)),
            dma((n,)),
            dma((total_n - 1,)),
            dma((parts, owners)),
            dma((out_pieces, total_n - 1)),
            dma((out_pieces, total_n)),
            dma,
            dma,
        ],
        compiler_params=pltpu.CompilerParams(
            collective_id=0, has_side_effects=True, vmem_limit_bytes=67043328
        ),
    )(
        tokens, gate_codes, gate_scales, up_codes, up_scales, down_codes, down_scales.reshape(1, width), hadamard,
    )
    return out


def fits(n, parts, tokens, gate_codes, gate_scales, down_codes):
    rows, depth = tokens.shape
    units, width = down_codes.shape
    return (
        rows == 1
        and parts == 2
        and n == ROWS
        and HA % n == 0
        and HA // n <= LANES // 2
        and HB <= LANES // 2
        and depth == gate_scales.shape[0] * LANES
        and depth % (ROWS * LANES * parts) == 0
        and width % (ROWS * LANES * parts) == 0
        and units % LANES == 0
        and units // LANES <= n
    )


def per_device(
    tokens, gate_codes, gate_scales, up_codes, up_scales, down_codes, down_scales, hadamard
):
    n = lax.axis_size("hx")
    parts = lax.axis_size("groups")
    if fits(n, parts, tokens, gate_codes, gate_scales, down_codes):
        return fused(
            n, parts, tokens, gate_codes, gate_scales, up_codes, up_scales, down_codes, down_scales, hadamard
        )
    gate_weight = dequantize(gate_codes, gate_scales)
    up_weight = dequantize(up_codes, up_scales)
    tile_rows = lax.all_gather(tokens, "hx", axis=0, tiled=True)
    gate = jnp.dot(tile_rows, gate_weight, preferred_element_type=jnp.float32)
    up_part = jnp.dot(tile_rows, up_weight, preferred_element_type=jnp.float32)
    hidden = jax.nn.silu(gate) * up_part
    factor = hadamard.astype(jnp.float32)
    gathered = lax.all_to_all(
        hidden.astype(jnp.bfloat16), "hx", split_axis=0, concat_axis=1, tiled=True
    ).astype(hidden.dtype)
    row_count = gathered.shape[0]
    cube = gathered.reshape(row_count, HA, HB)
    cube = jnp.einsum("tab,ac->tcb", cube, sylvester(HA), precision=lax.Precision.HIGHEST)
    cube = jnp.einsum("tcb,bd->tcd", cube, factor, precision=lax.Precision.HIGHEST)
    turned = lax.all_to_all(
        cube.reshape(row_count, FF).astype(jnp.bfloat16),
        "hx",
        split_axis=1,
        concat_axis=0,
        tiled=True,
    ).astype(jnp.float32)
    rotated = (turned * (1.0 / math.sqrt(FF))).astype(jnp.bfloat16)
    summed = lax.psum_scatter(
        jnp.dot(rotated, down_codes, preferred_element_type=jnp.float32),
        "hx",
        scatter_dimension=0,
        tiled=True,
    )
    mixed = (summed * down_scales[None, :]).astype(jnp.bfloat16)
    return mixed


def solution(mesh):
    in_specs = (
        P(("groups", "hx"), None),
        P(None, "hx"),
        P(None, "hx"),
        P(None, "hx"),
        P(None, "hx"),
        P("hx", None),
        P(),
        P(),
    )
    out_specs = P(("groups", "hx"), None)
    return jax.shard_map(
        per_device, mesh=mesh, in_specs=in_specs, out_specs=out_specs, check_vma=False
    )
```

```python
import functools
import math

import jax
import jax.numpy as jnp
from jax import lax
from jax.experimental import pallas as pl
from jax.experimental.pallas import tpu as pltpu
from jax.sharding import PartitionSpec as P

HA = 512
HB = 52
FF = 26624


def sylvester(size):
    index_vec = jnp.arange(size, dtype=jnp.int32)
    parity = jnp.zeros((size, size), jnp.int32)
    for level in range(max(size.bit_length() - 1, 0)):
        left_bits = jnp.right_shift(index_vec[:, None], level) & 1
        right_bits = jnp.right_shift(index_vec[None, :], level) & 1
        parity = parity + left_bits * right_bits
    return (1 - 2 * (parity % 2)).astype(jnp.float32)


def dequantize(codes, scales):
    row_total, col_total = codes.shape
    group_total = scales.shape[0]
    grouped = codes.astype(jnp.float32).reshape(group_total, row_total // group_total, col_total)
    return (grouped * scales[:, None, :]).reshape(row_total, col_total).astype(jnp.bfloat16)


LANES = 128
ROWS = 16
CHUNK_GROUPS = 4
SLOTS = 7


def kernel(
    n, tok_ref, gate_ref, gscale_ref, up_ref, uscale_ref, down_ref, dscale_ref, had_ref,
    out_ref,
    ring, gs, us, down, ds, had, corner, table, local, tok_row, tok_f32, tok_out_buf, tok, stage, lhs, acc, zbuf, recv_z, rbuf, rot, part, sendbuf, recv_c,
    ring_sem, load_sem, down_sem, tok_send, tok_recv, z_send, z_recv, r_send, r_recv, c_send, c_recv,
):
    me = lax.axis_index("hx")
    pieces = tok.shape[0]
    units = gate_ref.shape[1]
    owners = units // LANES
    chunk_rows = ring.shape[2]
    chunks = gate_ref.shape[0] // chunk_rows
    down_chunks, _, down_cols = down.shape
    out_pieces = recv_c.shape[0]
    peers = [lax.rem(me + step, n) for step in range(1, n)]

    def gate_copy(c, slot):
        rows = pl.ds(pl.multiple_of(c * chunk_rows, chunk_rows), chunk_rows)
        return pltpu.make_async_copy(gate_ref.at[rows], ring.at[slot, 0], ring_sem.at[slot, 0])

    def up_copy(c, slot):
        rows = pl.ds(pl.multiple_of(c * chunk_rows, chunk_rows), chunk_rows)
        return pltpu.make_async_copy(up_ref.at[rows], ring.at[slot, 1], ring_sem.at[slot, 1])

    def down_copy(c):
        cols = pl.ds(pl.multiple_of(c * down_cols, down_cols), down_cols)
        return pltpu.make_async_copy(down_ref.at[:, cols], down.at[c], down_sem.at[c])

    loads = [
        pltpu.make_async_copy(src, dst, load_sem.at[i])
        for i, (src, dst) in enumerate(
            ((tok_ref, tok_row), (had_ref, had), (dscale_ref, ds), (gscale_ref, gs), (uscale_ref, us))
        )
    ]

    barrier = pltpu.get_barrier_semaphore()
    for peer in peers:
        pl.semaphore_signal(barrier, inc=1, device_id={"hx": peer}, device_id_type=pl.DeviceIdType.MESH)
    for copy in loads:
        copy.start()
    for c in range(SLOTS):
        gate_copy(c, c).start()
        up_copy(c, c).start()
    loads[0].wait()
    row = tok_row[...].astype(jnp.float32)
    for k in range(pieces * ROWS):
        tok_f32[k : k + 1, :] = row[:, k * LANES : (k + 1) * LANES]
    tok_out_buf[...] = tok_f32[...].astype(jnp.bfloat16)
    for p in range(pieces):
        tok[p, me] = tok_out_buf[p * ROWS : (p + 1) * ROWS, :]
    loads[1].wait()

    half = LANES // 2
    hb = had.shape[0]
    ha = units // hb
    corner[...] = jnp.zeros_like(corner)
    corner[:hb, :hb] = had[...].astype(jnp.float32)
    left_bits = lax.broadcasted_iota(jnp.int32, (ha, ha), 0) & lax.broadcasted_iota(jnp.int32, (ha, ha), 1)
    parity = jnp.zeros((ha, ha), jnp.int32)
    for level in range(ha.bit_length() - 1):
        parity = parity ^ (jnp.right_shift(left_bits, level) & 1)
    corner[half : half + ha, half : half + ha] = (1 - 2 * parity).astype(jnp.float32)

    def digits(unit):
        high = jnp.floor((unit + 0.5) * (1.0 / hb))
        return high, unit - hb * high

    def wide(i, carry):
        shape = (LANES, LANES)
        unit = (lax.broadcasted_iota(jnp.int32, shape, 1) + i * LANES).astype(jnp.float32)
        at = lax.broadcasted_iota(jnp.int32, shape, 0).astype(jnp.float32)
        high, low = digits(unit)
        pick = jnp.where((at == low) | (at == high + half), 1.0, 0.0).astype(jnp.bfloat16)
        table[i] = jnp.dot(
            corner[...].astype(jnp.bfloat16), pick, preferred_element_type=jnp.float32
        ).astype(jnp.bfloat16)
        return carry

    lax.fori_loop(0, owners, wide, 0)
    factors = jnp.concatenate([table[j] for j in range(owners)], axis=1)

    def build(i, carry):
        shape = (LANES, LANES)
        unit = (lax.broadcasted_iota(jnp.int32, shape, 0) + i * LANES).astype(jnp.float32)
        at = lax.broadcasted_iota(jnp.int32, shape, 1).astype(jnp.float32)
        high, low = digits(unit)
        pick = jnp.concatenate(
            [jnp.where(at == low, 1.0, 0.0), jnp.where(at == high + half, 1.0, 0.0)], axis=0
        ).astype(jnp.bfloat16)
        both = jnp.dot(pick, factors, preferred_element_type=jnp.float32)
        rows = pl.ds(pl.multiple_of(i * LANES, LANES), LANES)
        local[rows, :] = (both[:LANES] * both[LANES:]).astype(jnp.bfloat16)
        return carry

    lax.fori_loop(0, owners // 2, build, 0)

    pl.semaphore_wait(barrier, n - 1)

    def remote(src, dst, send_sem, recv_sem, peer):
        return pltpu.make_async_remote_copy(
            src_ref=src, dst_ref=dst, send_sem=send_sem, recv_sem=recv_sem,
            device_id={"hx": peer}, device_id_type=pl.DeviceIdType.MESH,
        )

    def tok_out(p, i):
        return remote(
            tok_out_buf.at[pl.ds(p * ROWS, ROWS)], tok.at[p, me], tok_send.at[p, i], tok_recv.at[p, me], peers[i]
        )

    def tok_in(p, i):
        return remote(
            tok_out_buf.at[pl.ds(p * ROWS, ROWS)], tok.at[p, peers[i]], tok_send.at[p, i], tok_recv.at[p, peers[i]],
            peers[i],
        )

    for p in range(pieces):
        for i in range(n - 1):
            tok_out(p, i).start()

    lhs[...] = jnp.zeros_like(lhs)
    acc[...] = jnp.zeros_like(acc)
    lax.fori_loop(owners // 2, owners, build, 0)
    for copy in loads[2:]:
        copy.wait()

    pairs_piece = ROWS // 2
    chunks_piece = chunks // pieces
    pairs_chunk = CHUNK_GROUPS // 2
    for p in range(pieces):
        for i in range(n - 1):
            tok_in(p, i).wait_recv()
        stage[...] = tok[p].reshape(n * ROWS, LANES).astype(jnp.float32)
        for q in range(pairs_piece):
            lhs[q, :n, :LANES] = stage[pl.ds(2 * q, n, stride=ROWS), :].astype(jnp.bfloat16)
            lhs[q, n:, LANES:] = stage[pl.ds(2 * q + 1, n, stride=ROWS), :].astype(jnp.bfloat16)

        def step(k, carry):
            c = p * chunks_piece + k
            slot = lax.rem(c, SLOTS)
            gate_copy(c, slot).wait()
            up_copy(c, slot).wait()
            for q in range(pairs_chunk):
                left = lhs[k * pairs_chunk + q]
                row = c * CHUNK_GROUPS + 2 * q
                for w, scale in ((0, gs), (1, us)):
                    res = jnp.dot(
                        left, ring[slot, w, 2 * q * LANES : 2 * (q + 1) * LANES, :],
                        preferred_element_type=jnp.float32,
                    )
                    acc[w] += res[:n] * scale[pl.ds(row, 1), :] + res[n:] * scale[pl.ds(row + 1, 1), :]

            @pl.when(c + SLOTS < chunks)
            def _():
                gate_copy(c + SLOTS, slot).start()
                up_copy(c + SLOTS, slot).start()

            @pl.when(jnp.logical_and(c + SLOTS >= chunks, c + SLOTS - chunks < down_chunks))
            def _():
                down_copy(c + SLOTS - chunks).start()

            return carry

        lax.fori_loop(0, chunks_piece, step, 0)
    for c in range(SLOTS, down_chunks):
        down_copy(c).start()

    gate = acc[0]
    hidden = (gate / (1.0 + jnp.exp(-gate)) * acc[1]).astype(jnp.bfloat16)
    turned = jnp.dot(hidden, local[...], preferred_element_type=jnp.float32).astype(jnp.bfloat16)
    for j in range(owners):
        zbuf[j] = turned[:, j * LANES : (j + 1) * LANES]

    def z_out(j):
        return remote(zbuf.at[j], recv_z.at[me], z_send.at[j], z_recv.at[me], j)

    for j in range(owners):

        @pl.when(me != j)
        def _():
            z_out(j).start()

        @pl.when(me == j)
        def _():
            recv_z[j] = zbuf[j]

    def r_out(i):
        return remote(rbuf.at[peers[i]], rot.at[me], r_send.at[i], r_recv.at[me], peers[i])

    @pl.when(me < owners)
    def _():
        for i in range(n - 1):
            remote(zbuf.at[0], recv_z.at[peers[i]], z_send.at[0], z_recv.at[peers[i]], peers[i]).wait_recv()
        cube = [recv_z[h].astype(jnp.float32) for h in range(n)]
        span = 1
        while span < n:
            nxt = list(cube)
            for h in range(n):
                if h & span == 0:
                    nxt[h] = cube[h] + cube[h | span]
                    nxt[h | span] = cube[h] - cube[h | span]
            cube = nxt
            span *= 2
        for h in range(n):
            rbuf[h] = (cube[h] * (1.0 / math.sqrt(FF))).astype(jnp.bfloat16)
        for i in range(n - 1):
            r_out(i).start()
        rot[me] = rbuf[me]

    for j in range(owners):

        @pl.when(me != j)
        def _():
            remote(rbuf.at[0], rot.at[j], r_send.at[0], r_recv.at[j], j).wait_recv()

    rotated = jnp.concatenate([rot[j] for j in range(owners)], axis=1)

    def c_out(p, i):
        return remote(sendbuf.at[p, peers[i]], recv_c.at[p, me], c_send.at[p, i], c_recv.at[p, me], peers[i])

    def c_in(p, i):
        return remote(
            sendbuf.at[p, peers[i]], recv_c.at[p, peers[i]], c_send.at[p, i], c_recv.at[p, peers[i]], peers[i]
        )

    per_piece = down_chunks // out_pieces
    blocks = down_cols // LANES
    for p in range(out_pieces):
        for k in range(per_piece):
            c = p * per_piece + k
            down_copy(c).wait()
            res = jnp.dot(rotated, down[c], preferred_element_type=jnp.float32)
            for b in range(blocks):
                part[pl.ds(k * blocks + b, n, stride=ROWS), :] = res[:, b * LANES : (b + 1) * LANES]
        sendbuf[p] = part[...].astype(jnp.bfloat16).reshape(n, ROWS, LANES)
        for i in range(n - 1):
            c_out(p, i).start()
        recv_c[p, me] = sendbuf[p, me]

    for p in range(out_pieces):
        for i in range(n - 1):
            c_in(p, i).wait_recv()
        total = recv_c[p, 0].astype(jnp.float32)
        for h in range(1, n):
            total = total + recv_c[p, h].astype(jnp.float32)
        for r in range(ROWS):
            cols = slice((p * ROWS + r) * LANES, (p * ROWS + r + 1) * LANES)
            out_ref[:, cols] = (total[r : r + 1, :] * ds[:, cols]).astype(out_ref.dtype)

    for p in range(pieces):
        for i in range(n - 1):
            tok_out(p, i).wait_send()
    for j in range(owners):

        @pl.when(me != j)
        def _():
            z_out(j).wait_send()

    @pl.when(me < owners)
    def _():
        for i in range(n - 1):
            r_out(i).wait_send()

    for p in range(out_pieces):
        for i in range(n - 1):
            c_out(p, i).wait_send()


def fused(n, tokens, gate_codes, gate_scales, up_codes, up_scales, down_codes, down_scales, hadamard):
    depth, units = gate_codes.shape
    width = down_codes.shape[1]
    pieces = depth // (LANES * ROWS)
    out_pieces = width // (LANES * ROWS)
    owners = units // LANES
    chunk_rows = CHUNK_GROUPS * LANES
    down_cols = 8 * LANES
    bf16, f32 = jnp.bfloat16, jnp.float32
    dma = pltpu.SemaphoreType.DMA
    out = pl.pallas_call(
        functools.partial(kernel, n),
        out_shape=jax.ShapeDtypeStruct((1, width), bf16),
        in_specs=[pl.BlockSpec(memory_space=pl.ANY)] * 8,
        out_specs=pl.BlockSpec(memory_space=pltpu.VMEM),
        scratch_shapes=[
            pltpu.VMEM((SLOTS, 2, chunk_rows, units), bf16),
            pltpu.VMEM(gate_scales.shape, f32),
            pltpu.VMEM(up_scales.shape, f32),
            pltpu.VMEM((width // down_cols, units, down_cols), bf16),
            pltpu.VMEM((1, width), f32),
            pltpu.VMEM(hadamard.shape, hadamard.dtype),
            pltpu.VMEM((LANES, LANES), f32),
            pltpu.VMEM((owners, LANES, LANES), bf16),
            pltpu.VMEM((units, units), bf16),
            pltpu.VMEM((1, depth), bf16),
            pltpu.VMEM((depth // LANES, LANES), f32),
            pltpu.VMEM((depth // LANES, LANES), bf16),
            pltpu.VMEM((pieces, n, ROWS, LANES), bf16),
            pltpu.VMEM((n * ROWS, LANES), f32),
            pltpu.VMEM((ROWS // 2, 2 * n, 2 * LANES), bf16),
            pltpu.VMEM((2, n, units), f32),
            pltpu.VMEM((owners, n, LANES), bf16),
            pltpu.VMEM((n, n, LANES), bf16),
            pltpu.VMEM((n, n, LANES), bf16),
            pltpu.VMEM((owners, n, LANES), bf16),
            pltpu.VMEM((n * ROWS, LANES), f32),
            pltpu.VMEM((out_pieces, n, ROWS, LANES), bf16),
            pltpu.VMEM((out_pieces, n, ROWS, LANES), bf16),
            dma((SLOTS, 2)),
            dma((5,)),
            dma((width // down_cols,)),
            dma((pieces, n - 1)),
            dma((pieces, n)),
            dma((owners,)),
            dma((n,)),
            dma((n - 1,)),
            dma((owners,)),
            dma((out_pieces, n - 1)),
            dma((out_pieces, n)),
        ],
        compiler_params=pltpu.CompilerParams(
            collective_id=0, has_side_effects=True, vmem_limit_bytes=67043328
        ),
    )(
        tokens, gate_codes, gate_scales, up_codes, up_scales, down_codes, down_scales.reshape(1, width), hadamard,
    )
    return out


def fits(n, tokens, gate_codes, gate_scales, down_codes):
    rows, depth = tokens.shape
    units, width = down_codes.shape
    return (
        rows == 1
        and n == ROWS
        and HA % n == 0
        and HA // n <= LANES // 2
        and HB <= LANES // 2
        and depth == gate_scales.shape[0] * LANES
        and depth % (ROWS * LANES) == 0
        and width % (ROWS * LANES) == 0
        and units % LANES == 0
        and units // LANES <= n
    )


def per_device(
    tokens, gate_codes, gate_scales, up_codes, up_scales, down_codes, down_scales, hadamard
):
    n = lax.axis_size("hx")
    if fits(n, tokens, gate_codes, gate_scales, down_codes):
        return fused(
            n, tokens, gate_codes, gate_scales, up_codes, up_scales, down_codes, down_scales, hadamard
        )
    gate_weight = dequantize(gate_codes, gate_scales)
    up_weight = dequantize(up_codes, up_scales)
    tile_rows = lax.all_gather(tokens, "hx", axis=0, tiled=True)
    gate = jnp.dot(tile_rows, gate_weight, preferred_element_type=jnp.float32)
    up_part = jnp.dot(tile_rows, up_weight, preferred_element_type=jnp.float32)
    hidden = jax.nn.silu(gate) * up_part
    factor = hadamard.astype(jnp.float32)
    gathered = lax.all_to_all(
        hidden.astype(jnp.bfloat16), "hx", split_axis=0, concat_axis=1, tiled=True
    ).astype(hidden.dtype)
    row_count = gathered.shape[0]
    cube = gathered.reshape(row_count, HA, HB)
    cube = jnp.einsum("tab,ac->tcb", cube, sylvester(HA), precision=lax.Precision.HIGHEST)
    cube = jnp.einsum("tcb,bd->tcd", cube, factor, precision=lax.Precision.HIGHEST)
    turned = lax.all_to_all(
        cube.reshape(row_count, FF).astype(jnp.bfloat16),
        "hx",
        split_axis=1,
        concat_axis=0,
        tiled=True,
    ).astype(jnp.float32)
    rotated = (turned * (1.0 / math.sqrt(FF))).astype(jnp.bfloat16)
    summed = lax.psum_scatter(
        jnp.dot(rotated, down_codes, preferred_element_type=jnp.float32),
        "hx",
        scatter_dimension=0,
        tiled=True,
    )
    mixed = (summed * down_scales[None, :]).astype(jnp.bfloat16)
    return mixed


def solution(mesh):
    in_specs = (
        P(("groups", "hx"), None),
        P(None, "hx"),
        P(None, "hx"),
        P(None, "hx"),
        P(None, "hx"),
        P("hx", None),
        P(),
        P(),
    )
    out_specs = P(("groups", "hx"), None)
    return jax.shard_map(
        per_device, mesh=mesh, in_specs=in_specs, out_specs=out_specs, check_vma=False
    )
```
